32 devices in a mesh: pipe: 8 (over z, y), expert: 4 (over x, core).
Axes of the slice: x: 2, y: 2, z: 4, core: 2. Of those that a mesh axis runs over, the one named last changes fastest.
Arguments:
- first_input: bfloat16 [8, 256, 3072], P('pipe', 'expert'), may hold values from -6 to 6
- first_routes: int32 [8, 256, 2], P('pipe', 'expert'), may hold values from 0 to 7, as said below
- first_scores: float32 [8, 256, 2], P('pipe', 'expert'), may hold values from -6 to 6
- norm_gain: float32 [8, 3072], P('pipe'), may hold values from 0.5 to 1.5
- weight_in: bfloat16 [8, 2, 3072, 8192], P('pipe', None, None, 'expert'), may hold values from -0.109375 to 0.109375
- weight_out: bfloat16 [8, 8192, 3072], P('pipe', 'expert'), may hold values from -0.0625 to 0.0625
- second_grad: bfloat16 [8, 256, 3072], P('pipe', 'expert'), may hold values from -6 to 6
- second_routes: int32 [8, 256, 2], P('pipe', 'expert'), may hold values from 0 to 7, as said below
- second_scores: float32 [8, 256, 2], P('pipe', 'expert'), may hold values from -6 to 6
- second_stash: bfloat16 [8, 2, 80, 8192], P('pipe', None, None, 'expert'), may hold values from -5 to 5
Outputs:
- first_output: bfloat16 [8, 256, 3072], P('pipe', 'expert')
- input_grad: bfloat16 [8, 256, 3072], P('pipe', 'expert')
- mirror_stash: bfloat16 [8, 2, 80, 8192], P('pipe', None, None, 'expert')
The draws below stay inside these ranges and needn't reach their ends.
Inputs may be any that keep to these rules, and one draw needn't show every extreme that they name: `first_routes`: each row names two different experts. At each section, the 64 rows of one index of the expert axis name expert 0 between 2 and 20 times, and at every section some index names it exactly 20 times. `second_routes`: as for first_routes.
All inputs are finite; a program needn't handle non-finite values.
Results may differ from the reference program's by a relative error of at most 0.0058.
Values may be sent and summed in bfloat16 or wider, within the bound.
No kernel may reach another device: no remote copies, remote signals or barrier semaphores. Data moves between devices by JAX's collectives and lax.ppermute only.
A program may use at most 128 MiB of HBM per device.

```python
import jax
import jax.numpy as jnp
from jax import lax

D = 3072
FF = 8192
EXPERTS = 8
TOK = 64
CAP = 20
ROWS = 80
TOKENS = 256
N_PIPE = 8
N_EXPERT = 4


def shuffled_rows(order_key):
    return jax.random.permutation(order_key, TOK)


def route_pairs(key):
    count_key, full_key, order_key, chosen_key, offset_key, flip_key = jax.random.split(key, 6)
    span = CAP - 1
    factors = jax.random.randint(count_key, (2, N_PIPE, N_EXPERT), 0, span)
    window_count = jnp.minimum(2 + factors[0] * factors[1] // max(span - 1, 1), CAP)
    full_at = jax.random.randint(full_key, (N_PIPE, 1), 0, N_EXPERT)
    window_count = jnp.where(jnp.arange(N_EXPERT, dtype=jnp.int32)[None, :] == full_at, CAP, window_count)
    order_keys = jax.random.split(order_key, N_PIPE * N_EXPERT)
    row_order = jax.vmap(shuffled_rows)(order_keys).reshape(N_PIPE, N_EXPERT, TOK)
    routed = row_order < window_count[..., None]
    chosen = jax.random.randint(chosen_key, (N_PIPE, N_EXPERT, TOK), 1, EXPERTS)
    offset = jax.random.randint(offset_key, (N_PIPE, N_EXPERT, TOK), 1, EXPERTS - 1)
    partner = 1 + (chosen - 1 + offset) % (EXPERTS - 1)
    leading = jnp.where(routed, 0, chosen)
    trailing = jnp.where(routed, chosen, partner)
    flipped = jax.random.randint(flip_key, (N_PIPE, N_EXPERT, TOK), 0, 2) == 1
    column_one = jnp.where(flipped, trailing, leading)
    column_two = jnp.where(flipped, leading, trailing)
    return jnp.stack([column_one, column_two], axis=-1).reshape(N_PIPE, N_EXPERT * TOK, 2).astype(jnp.int32)


def draw_first_routes(key, part):
    return route_pairs(jax.random.fold_in(key, 11))


def draw_second_routes(key, part):
    return route_pairs(jax.random.fold_in(key, 23))


def shard_levels(stream_key, shape, cuts, smallest, high):
    factor_of = 1.0
    for position, shards_of in cuts:
        heights = jax.random.uniform(jax.random.fold_in(jax.random.fold_in(stream_key, 6), position), (shards_of,), jnp.float32, smallest / len(cuts), high / len(cuts))
        factor_of = factor_of * jnp.repeat(jnp.exp(heights), shape[position] // shards_of).reshape((-1,) + (1,) * (len(shape) - 1 - position))
    return factor_of


def noise(key, shape, deviation, limit, cuts=(), kind=jnp.bfloat16):
    factor_of = shard_levels(key, shape, cuts, -0.22, 0.18) if cuts else 1.0
    entries = jax.random.normal(key, shape, jnp.float32) * deviation * factor_of
    return jnp.minimum(jnp.maximum(entries, -limit), limit).astype(kind)


def setup_inputs(seed: int = 0) -> dict:
    seeds = jax.random.split(jax.random.key(seed), 11)
    first_input = noise(seeds[0], (N_PIPE, TOKENS, D), 1.0, 6.0, ((0, 8), (1, 4)))
    first_routes = draw_first_routes(jax.random.fold_in(seeds[10], 71), 0)
    first_scores = noise(seeds[2], (N_PIPE, TOKENS, 2), 1.5, 6.0, ((0, 8), (1, 4)), jnp.float32)
    norm_gain = jnp.clip(1.0 + 0.1 * jax.random.normal(seeds[3], (N_PIPE, D), jnp.float32), 0.5, 1.5)
    weight_in = noise(seeds[4], (N_PIPE, 2, D, FF), D ** -0.5, 0.109375, ((0, 8), (3, 4)))
    weight_out = noise(seeds[5], (N_PIPE, FF, D), FF ** -0.5, 0.0625, ((0, 8), (1, 4)))
    second_grad = noise(seeds[6], (N_PIPE, TOKENS, D), 1.0, 6.0, ((0, 8), (1, 4)))
    second_routes = draw_second_routes(jax.random.fold_in(seeds[10], 71), 0)
    second_scores = noise(seeds[8], (N_PIPE, TOKENS, 2), 1.5, 6.0, ((0, 8), (1, 4)), jnp.float32)
    second_stash = noise(seeds[9], (N_PIPE, 2, ROWS, FF), 1.0, 5.0, ((0, 8), (3, 4)))
    return dict(first_input=first_input, first_routes=first_routes, first_scores=first_scores, norm_gain=norm_gain, weight_in=weight_in, weight_out=weight_out, second_grad=second_grad, second_routes=second_routes, second_scores=second_scores, second_stash=second_stash)


EPSILON = 1e-05

def block_select(routes, scores):
    route_flags = (routes == 0).astype(jnp.int32)
    flag_line = route_flags.reshape(-1)
    earlier = (jnp.cumsum(flag_line) - flag_line).reshape(route_flags.shape)
    token_routed = lax.optimization_barrier(jnp.sum(route_flags, axis=1))
    token_slot = (lax.optimization_barrier(jnp.sum(earlier * route_flags, axis=1)) + (1 - token_routed) * CAP).astype(jnp.int32)
    differ = scores[:, 0] - scores[:, 1]
    pair_weight = jnp.stack([jax.nn.sigmoid(differ), jax.nn.sigmoid(-differ)], axis=1)
    token_weight = lax.optimization_barrier(jnp.sum(route_flags.astype(jnp.float32) * pair_weight, axis=1))
    selector = (jnp.arange(CAP, dtype=jnp.int32)[:, None] == token_slot[None, :]).astype(jnp.float32)
    return (selector, token_weight)

def section_window(section_items):
    first_input, first_routes, first_scores, norm_gain, weight_in, weight_out, second_grad, second_routes, second_scores, stash_used = section_items
    wide_in = first_input.astype(jnp.float32)
    normed = (wide_in * lax.rsqrt(lax.optimization_barrier(jnp.mean(wide_in * wide_in, axis=-1, keepdims=True)) + EPSILON) * norm_gain).astype(jnp.bfloat16)
    first_select, first_weight = jax.vmap(block_select)(first_routes.reshape(N_EXPERT, TOK, 2), first_scores.reshape(N_EXPERT, TOK, 2))
    blocks = normed.reshape(N_EXPERT, TOK, D).astype(jnp.float32)
    dispatched = jnp.einsum('sct,std->scd', first_select, blocks).astype(jnp.bfloat16).reshape(ROWS, D)
    gate_rows = jnp.dot(dispatched, weight_in[0], preferred_element_type=jnp.float32)
    up_rows = jnp.dot(dispatched, weight_in[1], preferred_element_type=jnp.float32)
    stash_made = jnp.stack([gate_rows, up_rows]).astype(jnp.bfloat16)
    hidden = (jax.nn.silu(gate_rows) * up_rows).astype(jnp.bfloat16)
    expert_out = jnp.dot(hidden, weight_out, preferred_element_type=jnp.float32).astype(jnp.bfloat16)
    picked = jnp.einsum('sct,scd->std', first_select, expert_out.reshape(N_EXPERT, CAP, D).astype(jnp.float32))
    first_output = (wide_in + (first_weight.reshape(N_EXPERT, TOK, 1) * picked).reshape(TOKENS, D)).astype(jnp.bfloat16)
    second_select, second_weight = jax.vmap(block_select)(second_routes.reshape(N_EXPERT, TOK, 2), second_scores.reshape(N_EXPERT, TOK, 2))
    scaled = (second_grad.astype(jnp.float32).reshape(N_EXPERT, TOK, D) * second_weight.reshape(N_EXPERT, TOK, 1)).astype(jnp.bfloat16)
    grad_slots = jnp.einsum('sct,std->scd', second_select, scaled.astype(jnp.float32)).astype(jnp.bfloat16).reshape(ROWS, D)
    gate_part = stash_used[0].astype(jnp.float32)
    up_part = stash_used[1].astype(jnp.float32)
    grad_hidden = jnp.dot(grad_slots, weight_out.T, preferred_element_type=jnp.float32)
    sigmoid_gate = jax.nn.sigmoid(gate_part)
    swish_slope = sigmoid_gate * (1.0 + gate_part * (1.0 - sigmoid_gate))
    grad_gate = (grad_hidden * up_part * swish_slope).astype(jnp.bfloat16)
    grad_up = (grad_hidden * (gate_part * sigmoid_gate)).astype(jnp.bfloat16)
    grad_rows = (jnp.dot(grad_gate, weight_in[0].T, preferred_element_type=jnp.float32) + jnp.dot(grad_up, weight_in[1].T, preferred_element_type=jnp.float32)).astype(jnp.bfloat16)
    input_grad = jnp.einsum('sct,scd->std', second_select, grad_rows.reshape(N_EXPERT, CAP, D).astype(jnp.float32))
    input_grad = input_grad.reshape(TOKENS, D).astype(jnp.bfloat16)
    return (first_output, input_grad, stash_made)

def reference(first_input, first_routes, first_scores, norm_gain, weight_in, weight_out, second_grad, second_routes, second_scores, second_stash):
    fetched = jnp.roll(second_stash, N_PIPE // 2, axis=0)
    first_output, input_grad, stash_made = lax.map(section_window, (first_input, first_routes, first_scores, norm_gain, weight_in, weight_out, second_grad, second_routes, second_scores, fetched))
    return (first_output, input_grad, jnp.roll(stash_made, N_PIPE // 2, axis=0))
```

```python
import jax
import jax.numpy as jnp
from jax import lax
from jax.sharding import PartitionSpec as P

EPSILON = 1e-05
F32 = jnp.float32
BF16 = jnp.bfloat16


def partner(shard, axis, apart):
    return lax.ppermute(shard, axis, [(i, i ^ (1 << apart)) for i in range(lax.axis_size(axis))])


def bits_of(axis):
    return lax.axis_size(axis).bit_length() - 1


def gather_blocks(block, axis):
    me = lax.axis_index(axis)
    held = block
    for bit in reversed(range(bits_of(axis))):
        other = partner(held, axis, bit)
        mine_low = (me >> bit) & 1 == 0
        held = jnp.stack([jnp.where(mine_low, held, other), jnp.where(mine_low, other, held)], axis=1)
        held = held.reshape((-1,) + block.shape[1:])
    return held


def scatter_blocks(parts, axis):
    me = lax.axis_index(axis)
    held = parts
    for bit in range(bits_of(axis)):
        split = held.reshape((-1, 2) + held.shape[1:])
        mine = (me >> bit) & 1
        keep = lax.dynamic_index_in_dim(split, mine, 1, keepdims=False)
        send = lax.dynamic_index_in_dim(split, 1 - mine, 1, keepdims=False)
        held = keep + partner(send.astype(BF16), axis, bit).astype(F32)
    return held


def block_select(routes, scores, capacity):
    routed = jnp.any(routes == 0, axis=1)
    tokens = routes.shape[0]
    step = jnp.arange(tokens, dtype=jnp.int32)
    before = (step[:, None] < step[None, :]) & routed[:, None]
    slot = jnp.sum(before.astype(jnp.int32), axis=0)
    slot = jnp.where(routed, slot, capacity)
    differ = scores[:, 0] - scores[:, 1]
    weight = jnp.where(
        routes[:, 0] == 0, jax.nn.sigmoid(differ), jnp.where(routes[:, 1] == 0, jax.nn.sigmoid(-differ), 0.0)
    )
    selector = (jnp.arange(capacity, dtype=jnp.int32)[:, None] == slot[None, :]).astype(BF16)
    return (selector, weight)


def body(
    first_input,
    first_routes,
    first_scores,
    norm_gain,
    weight_in,
    weight_out,
    second_grad,
    second_routes,
    second_scores,
    second_stash,
):
    size = lax.axis_size("expert")
    capacity = second_stash.shape[2] // size
    local_gate = weight_in[0, 0]
    local_up = weight_in[0, 1]
    local_out = weight_out[0]
    width = first_input.shape[2]
    top_bit = bits_of("pipe") - 1
    along_rows = (((0,), (0,)), ((), ()))
    along_cols = (((1,), (1,)), ((), ()))
    fetched = partner(second_stash, "pipe", top_bit)
    wide_in = first_input[0].astype(F32)
    normed = (
        wide_in * lax.rsqrt(jnp.mean(wide_in * wide_in, axis=-1, keepdims=True) + EPSILON) * norm_gain[0]
    ).astype(BF16)
    first_select, first_weight = block_select(first_routes[0], first_scores[0], capacity)
    second_select, second_weight = block_select(second_routes[0], second_scores[0], capacity)
    send_first = jnp.dot(first_select, normed, preferred_element_type=F32).astype(BF16)
    scaled = (second_grad[0].astype(F32) * second_weight[:, None]).astype(BF16)
    send_second = jnp.dot(second_select, scaled, preferred_element_type=F32).astype(BF16)

    rows = gather_blocks(send_first[None], "expert").reshape(-1, width)
    rows_second = gather_blocks(send_second[None], "expert").reshape(-1, width)
    gate_rows = jnp.dot(rows, local_gate, preferred_element_type=F32)
    up_rows = jnp.dot(rows, local_up, preferred_element_type=F32)
    stash_made = jnp.stack([gate_rows, up_rows]).astype(BF16)
    mirror = partner(stash_made[None], "pipe", top_bit)
    hidden = (jax.nn.silu(gate_rows) * up_rows).astype(BF16)
    out_part = jnp.dot(hidden, local_out, preferred_element_type=F32)
    expert_out = scatter_blocks(out_part.reshape(size, capacity, width), "expert")[0].astype(BF16)

    grad_hidden = lax.dot_general(rows_second, local_out, along_cols, preferred_element_type=F32)
    gate_part = fetched[0, 0].astype(F32)
    up_part = fetched[0, 1].astype(F32)
    sigmoid_gate = jax.nn.sigmoid(gate_part)
    swish_slope = sigmoid_gate * (1.0 + gate_part * (1.0 - sigmoid_gate))
    grad_gate = (grad_hidden * up_part * swish_slope).astype(BF16)
    grad_up = (grad_hidden * (gate_part * sigmoid_gate)).astype(BF16)
    grad_part = lax.dot_general(grad_gate, local_gate, along_cols, preferred_element_type=F32) + lax.dot_general(
        grad_up, local_up, along_cols, preferred_element_type=F32
    )
    grad_rows = scatter_blocks(grad_part.reshape(size, capacity, width), "expert")[0].astype(BF16)

    picked = lax.dot_general(first_select, expert_out, along_rows, preferred_element_type=F32)
    first_output = (wide_in + first_weight[:, None] * picked).astype(BF16)
    input_grad = lax.dot_general(second_select, grad_rows, along_rows, preferred_element_type=F32).astype(BF16)
    return (first_output[None], input_grad[None], mirror)


def solution(mesh):
    tokens = P("pipe", "expert", None)
    columns = P("pipe", None, None, "expert")
    return jax.shard_map(
        body,
        mesh=mesh,
        in_specs=(
            tokens,
            tokens,
            tokens,
            P("pipe", None),
            columns,
            tokens,
            tokens,
            tokens,
            tokens,
            columns,
        ),
        out_specs=(tokens, tokens, columns),
        check_vma=False,
    )
```

```python
import functools

import jax
import jax.numpy as jnp
from jax import lax
from jax.experimental import pallas as pl
from jax.experimental.pallas import tpu as pltpu
from jax.sharding import PartitionSpec as P

EPSILON = 1e-05
F32 = jnp.float32
BF16 = jnp.bfloat16
I32 = jnp.int32
ALONG_ROWS = (((0,), (0,)), ((), ()))
ALONG_COLS = (((1,), (1,)), ((), ()))
VMEM = pl.BlockSpec(memory_space=pltpu.VMEM)
SMEM = pl.BlockSpec(memory_space=pltpu.SMEM)


def dot(a, b, dims=None):
    return lax.dot_general(a, b, dims or (((1,), (0,)), ((), ())), preferred_element_type=F32)


def partner(shard, axis, apart):
    return lax.ppermute(shard, axis, [(i, i ^ (1 << apart)) for i in range(lax.axis_size(axis))])


def bits_of(axis):
    return lax.axis_size(axis).bit_length() - 1


def tile_of(length, most):
    return max(t for t in range(128, min(length, most) + 1, 128) if length % t == 0)


def gather_blocks(block, axis):
    me = lax.axis_index(axis)
    held = block
    for bit in reversed(range(bits_of(axis))):
        other = partner(held, axis, bit)
        mine_low = (me >> bit) & 1 == 0
        held = jnp.stack([jnp.where(mine_low, held, other), jnp.where(mine_low, other, held)], axis=1)
        held = held.reshape((-1,) + block.shape[1:])
    return held


def scatter_rest(held, axis, first_bit):
    me = lax.axis_index(axis)
    for bit in range(first_bit, bits_of(axis)):
        split = held.reshape((-1, 2) + held.shape[1:])
        mine = (me >> bit) & 1
        keep = lax.dynamic_index_in_dim(split, mine, 1, keepdims=False)
        send = lax.dynamic_index_in_dim(split, 1 - mine, 1, keepdims=False)
        held = keep.astype(F32) + partner(send.astype(BF16), axis, bit).astype(F32)
    return held


def block_select(routes, scores, capacity):
    routed = jnp.any(routes == 0, axis=1)
    tokens = routes.shape[0]
    step = jnp.arange(tokens, dtype=I32)
    before = (step[:, None] < step[None, :]) & routed[:, None]
    slot = jnp.where(routed, jnp.sum(before.astype(I32), axis=0), capacity)
    differ = scores[:, 0] - scores[:, 1]
    weight = jnp.where(
        routes[:, 0] == 0, jax.nn.sigmoid(differ), jnp.where(routes[:, 1] == 0, jax.nn.sigmoid(-differ), 0.0)
    )
    selector = (jnp.arange(capacity, dtype=I32)[:, None] == slot[None, :]).astype(BF16)
    return (selector, weight)


def selector_of(routes, capacity):
    tokens = routes.shape[0]
    routed = jnp.max((routes == 0).astype(F32), axis=1, keepdims=True)
    row = lax.broadcasted_iota(I32, (tokens, tokens), 0)
    col = lax.broadcasted_iota(I32, (tokens, tokens), 1)
    slot = jnp.sum(jnp.where(row < col, routed, 0.0), axis=0, keepdims=True)
    here = jnp.sum(jnp.where(row == col, routed, 0.0), axis=0, keepdims=True)
    slot = jnp.where(here > 0.0, slot, float(capacity)).astype(I32)
    return jnp.where(lax.broadcasted_iota(I32, (capacity, tokens), 0) == slot, 1.0, 0.0).astype(BF16)


def packing(counts, base, blocks, capacity, early, spill, late_only=False, early_only=False):
    head = blocks * early
    first = head if late_only else 0
    rows = (head if early_only else head + spill) - first
    row = lax.broadcasted_iota(I32, (rows, blocks * capacity), 0) + first
    col = lax.broadcasted_iota(I32, (rows, blocks * capacity), 1)
    hit = None
    offset = head
    for s in range(blocks):
        slot = col - s * capacity
        tests = []
        if not late_only:
            tests.append((slot >= 0) & (slot < early) & (row == s * early + slot))
        if not early_only:
            count = counts[base + s]
            tests.append((slot >= early) & (slot < count) & (row == slot + (offset - early)) & (row >= head))
            offset = offset + jnp.maximum(count - early, 0)
        for test in tests:
            hit = test if hit is None else hit | test
    return jnp.where(hit, 1.0, 0.0).astype(BF16)


def store_split(value, keep_ref, send_ref, parity, capacity, columns):
    blocks = value.shape[0] // capacity
    for s in range(blocks):
        block = value[s * capacity : (s + 1) * capacity]

        @pl.when(parity == s % 2)
        def _():
            keep_ref[s // 2, :, columns] = block

        @pl.when(parity != s % 2)
        def _():
            send_ref[s // 2, :, columns] = block


def early_kernel(blocks, capacity, early, spill, stash_ref, out_ref):
    pick = packing(None, 0, blocks, capacity, early, spill, early_only=True)
    for g in range(2):
        out_ref[g] = dot(pick, stash_ref[g]).astype(BF16)


def late_kernel(blocks, capacity, early, spill, counts_ref, stash_ref, out_ref):
    pick = packing(counts_ref, 3 * blocks, blocks, capacity, early, spill, late_only=True)
    for g in range(2):
        out_ref[g] = dot(pick, stash_ref[g]).astype(BF16)


def first_kernel(input_ref, gain_ref, routes_ref, second_routes_ref, out_ref, counts_ref):
    wide = input_ref[...].astype(F32)
    scale = lax.rsqrt(jnp.mean(wide * wide, axis=-1, keepdims=True) + EPSILON)
    normed = (wide * scale * gain_ref[...]).astype(BF16)
    out_ref[...] = dot(selector_of(routes_ref[...], out_ref.shape[0]), normed).astype(BF16)
    counts_ref[0:1, :] = jnp.broadcast_to(jnp.sum((routes_ref[...] == 0).astype(I32)), (1, counts_ref.shape[1]))
    counts_ref[1:2, :] = jnp.broadcast_to(
        jnp.sum((second_routes_ref[...] == 0).astype(I32)), (1, counts_ref.shape[1])
    )


def second_kernel(grad_ref, routes_ref, scores_ref, out_ref):
    routes = routes_ref[...]
    differ = scores_ref[:, 0:1] - scores_ref[:, 1:2]
    weight = jnp.where(
        routes[:, 0:1] == 0, jax.nn.sigmoid(differ), jnp.where(routes[:, 1:2] == 0, jax.nn.sigmoid(-differ), 0.0)
    )
    scaled = (grad_ref[...].astype(F32) * weight).astype(BF16)
    out_ref[...] = dot(selector_of(routes, out_ref.shape[0]), scaled).astype(BF16)


def gate_up_kernel(blocks, capacity, early, spill, counts_ref, rows_ref, weight_ref, packed_ref, hidden_ref, pick_ref):
    @pl.when(pl.program_id(0) == 0)
    def _():
        pick_ref[...] = packing(counts_ref, 0, blocks, capacity, early, spill)

    rows = rows_ref[...]
    gate = dot(rows, weight_ref[0])
    up = dot(rows, weight_ref[1])
    hidden_ref[...] = (gate * jax.nn.sigmoid(gate) * up).astype(BF16)
    packed_ref[0] = dot(pick_ref[...], gate.astype(BF16)).astype(BF16)
    packed_ref[1] = dot(pick_ref[...], up.astype(BF16)).astype(BF16)


def out_kernel(
    blocks,
    capacity,
    early,
    spill,
    counts_ref,
    hidden_ref,
    rows_ref,
    weight_ref,
    keep_ref,
    send_ref,
    grad_hidden_ref,
    total_ref,
    packed_ref,
):
    step = pl.program_id(0)

    @pl.when(step == 0)
    def _():
        pick = packing(counts_ref, blocks, blocks, capacity, early, spill)
        packed_ref[...] = dot(pick, rows_ref[...]).astype(BF16)
        total_ref[...] = jnp.zeros_like(total_ref)

    weight = weight_ref[...]
    grad_hidden_ref[...] = dot(packed_ref[...], weight, ALONG_COLS)
    total_ref[...] += dot(hidden_ref[...], weight)

    @pl.when(step == pl.num_programs(0) - 1)
    def _():
        store_split(total_ref[...].astype(BF16), keep_ref, send_ref, counts_ref[4 * blocks] % 2, capacity, slice(None))


def grads_kernel(
    blocks,
    capacity,
    early,
    spill,
    counts_ref,
    early_ref,
    late_ref,
    grad_hidden_ref,
    weight_ref,
    keep_ref,
    send_ref,
    grad_gate_ref,
    grad_up_ref,
    pick_ref,
):
    @pl.when(pl.program_id(0) == 0)
    def _():
        pick_ref[...] = packing(counts_ref, blocks, blocks, capacity, early, spill)
        head = blocks * early
        for part, rows in ((early_ref, slice(0, head)), (late_ref, slice(head, head + spill))):
            gate = part[0].astype(F32)
            up = part[1].astype(F32)
            grad_hidden = grad_hidden_ref[rows]
            q = jax.nn.sigmoid(gate)
            grad_gate_ref[rows] = (grad_hidden * up * (q * (1.0 + gate * (1.0 - q)))).astype(BF16)
            grad_up_ref[rows] = (grad_hidden * (gate * q)).astype(BF16)

    part = dot(grad_gate_ref[...], weight_ref[0], ALONG_COLS) + dot(grad_up_ref[...], weight_ref[1], ALONG_COLS)
    rows = dot(pick_ref[...], part.astype(BF16), ALONG_ROWS).astype(BF16)
    store_split(rows, keep_ref, send_ref, counts_ref[4 * blocks] % 2, capacity, slice(None))


def unpack_kernel(blocks, capacity, early, spill, counts_ref, packed_ref, out_ref):
    pick = packing(counts_ref, 2 * blocks, blocks, capacity, early, spill)
    out_ref[...] = dot(pick, packed_ref[...], ALONG_ROWS).astype(BF16)


def body(
    first_input,
    first_routes,
    first_scores,
    norm_gain,
    weight_in,
    weight_out,
    second_grad,
    second_routes,
    second_scores,
    second_stash,
):
    blocks = lax.axis_size("expert")
    me = lax.axis_index("expert")
    rows_all, units = second_stash.shape[2:]
    width = first_input.shape[2]
    capacity = rows_all // blocks
    early = capacity * 2 // 5
    spill = blocks * early
    packed_rows = blocks * early + spill
    plan = (blocks, capacity, early, spill)
    top_bit = bits_of("pipe") - 1
    stash_in = second_stash[0]
    weights_in = weight_in[0]
    weights_out = weight_out[0]

    early_rows = pl.pallas_call(
        functools.partial(early_kernel, *plan),
        out_shape=jax.ShapeDtypeStruct((2, blocks * early, units), BF16),
        in_specs=[VMEM],
        out_specs=VMEM,
        name="pack_early",
    )(stash_in)
    fetched_early = partner(early_rows, "pipe", top_bit)

    send_first, counts = pl.pallas_call(
        first_kernel,
        out_shape=(
            jax.ShapeDtypeStruct((capacity, width), BF16),
            jax.ShapeDtypeStruct((2, blocks), I32),
        ),
        in_specs=[VMEM] * 4,
        out_specs=(VMEM, VMEM),
        name="select_first",
    )(first_input[0], norm_gain, first_routes[0], second_routes[0])
    mine = jnp.where(jnp.arange(blocks, dtype=I32)[None, :] == me, counts, 0)
    tally = jnp.stack([mine, partner(mine, "pipe", top_bit)])
    for bit in reversed(range(bits_of("expert"))):
        tally = tally + partner(tally, "expert", bit)
    info = jnp.concatenate([tally.reshape(-1), me.astype(I32)[None]])
    send_second = pl.pallas_call(
        second_kernel,
        out_shape=jax.ShapeDtypeStruct((capacity, width), BF16),
        in_specs=[VMEM] * 3,
        out_specs=VMEM,
        name="select_second",
    )(second_grad[0], second_routes[0], second_scores[0])
    rows = gather_blocks(send_first[None], "expert").reshape(-1, width)
    rows_second = gather_blocks(send_second[None], "expert").reshape(-1, width)

    late_rows = pl.pallas_call(
        functools.partial(late_kernel, *plan),
        out_shape=jax.ShapeDtypeStruct((2, spill, units), BF16),
        in_specs=[SMEM, VMEM],
        out_specs=VMEM,
        name="pack_late",
    )(info, stash_in)
    fetched_late = partner(late_rows, "pipe", top_bit)

    over = jnp.max(jnp.sum(jnp.maximum(tally - early, 0), axis=-1) - spill).reshape(1)
    for bit in range(top_bit):
        over = jnp.maximum(over, partner(over, "pipe", bit))

    tile = tile_of(units, 256)
    packed, hidden = pl.pallas_call(
        functools.partial(gate_up_kernel, *plan),
        grid=(units // tile,),
        out_shape=(
            jax.ShapeDtypeStruct((2, packed_rows, units), BF16),
            jax.ShapeDtypeStruct((rows_all, units), BF16),
        ),
        in_specs=[
            SMEM,
            pl.BlockSpec((rows_all, width), lambda i: (0, 0)),
            pl.BlockSpec((2, width, tile), lambda i: (0, 0, i)),
        ],
        out_specs=(
            pl.BlockSpec((2, packed_rows, tile), lambda i: (0, 0, i)),
            pl.BlockSpec((rows_all, tile), lambda i: (0, i)),
        ),
        scratch_shapes=[pltpu.VMEM((packed_rows, rows_all), BF16)],
        cost_estimate=pl.CostEstimate(
            flops=4 * rows_all * width * units, bytes_accessed=4 * width * units, transcendentals=0
        ),
        name="gate_up",
    )(info, rows, weights_in)
    mirror_packed = partner(packed, "pipe", top_bit)

    tile = tile_of(units, 256)
    half = (blocks // 2, capacity, width)
    whole = lambda shape: pl.BlockSpec(shape, lambda i: (0,) * len(shape))
    out_keep, out_send, grad_hidden = pl.pallas_call(
        functools.partial(out_kernel, *plan),
        grid=(units // tile,),
        out_shape=(
            jax.ShapeDtypeStruct(half, BF16),
            jax.ShapeDtypeStruct(half, BF16),
            jax.ShapeDtypeStruct((packed_rows, units), F32),
        ),
        in_specs=[
            SMEM,
            pl.BlockSpec((rows_all, tile), lambda i: (0, i)),
            whole((rows_all, width)),
            pl.BlockSpec((tile, width), lambda i: (i, 0)),
        ],
        out_specs=(whole(half), whole(half), pl.BlockSpec((packed_rows, tile), lambda i: (0, i))),
        scratch_shapes=[pltpu.VMEM((rows_all, width), F32), pltpu.VMEM((packed_rows, width), BF16)],
        cost_estimate=pl.CostEstimate(
            flops=4 * rows_all * width * units, bytes_accessed=2 * width * units, transcendentals=0
        ),
        name="out_and_grad_hidden",
    )(info, hidden, rows_second, weights_out)
    expert_out = scatter_rest(
        out_keep.astype(F32) + partner(out_send, "expert", 0).astype(F32), "expert", 1
    )[0].astype(BF16)
    first_select, first_weight = block_select(first_routes[0], first_scores[0], capacity)
    picked = dot(first_select, expert_out, ALONG_ROWS)
    first_output = (first_input[0].astype(F32) + first_weight[:, None] * picked).astype(BF16)

    tile = tile_of(width, 384)
    split = pl.BlockSpec((blocks // 2, capacity, tile), lambda i: (0, 0, i))
    grad_keep, grad_send = pl.pallas_call(
        functools.partial(grads_kernel, *plan),
        grid=(width // tile,),
        out_shape=(jax.ShapeDtypeStruct(half, BF16), jax.ShapeDtypeStruct(half, BF16)),
        in_specs=[
            SMEM,
            whole((2, blocks * early, units)),
            whole((2, spill, units)),
            whole((packed_rows, units)),
            pl.BlockSpec((2, tile, units), lambda i: (0, i, 0)),
        ],
        out_specs=(split, split),
        scratch_shapes=[
            pltpu.VMEM((packed_rows, units), BF16),
            pltpu.VMEM((packed_rows, units), BF16),
            pltpu.VMEM((packed_rows, rows_all), BF16),
        ],
        cost_estimate=pl.CostEstimate(
            flops=4 * packed_rows * width * units, bytes_accessed=4 * width * units, transcendentals=0
        ),
        name="grads",
    )(info, fetched_early, fetched_late, grad_hidden, weights_in)
    grad_rows = scatter_rest(
        grad_keep.astype(F32) + partner(grad_send, "expert", 0).astype(F32), "expert", 1
    )[0].astype(BF16)
    second_select, _ = block_select(second_routes[0], second_scores[0], capacity)

    def packed_case(grad_rows, packed, info):
        tile = tile_of(units, 1024)
        mirror = pl.pallas_call(
            functools.partial(unpack_kernel, *plan),
            grid=(2, units // tile),
            out_shape=jax.ShapeDtypeStruct((2, rows_all, units), BF16),
            in_specs=[SMEM, pl.BlockSpec((None, packed_rows, tile), lambda g, i: (g, 0, i))],
            out_specs=pl.BlockSpec((None, rows_all, tile), lambda g, i: (g, 0, i)),
            name="unpack",
        )(info, packed)
        return (dot(second_select, grad_rows, ALONG_ROWS).astype(BF16)[None], mirror[None])

    def full_case(grad_rows, packed, info):
        fetched = partner(stash_in, "pipe", top_bit)
        gate = dot(rows, weights_in[0])
        up = dot(rows, weights_in[1])
        mirror = partner(jnp.stack([gate, up]).astype(BF16), "pipe", top_bit)
        grad_hidden = dot(rows_second, weights_out, ALONG_COLS)
        gate = fetched[0].astype(F32)
        up = fetched[1].astype(F32)
        q = jax.nn.sigmoid(gate)
        grad_gate = (grad_hidden * up * (q * (1.0 + gate * (1.0 - q)))).astype(BF16)
        grad_up = (grad_hidden * (gate * q)).astype(BF16)
        parts = dot(grad_gate, weights_in[0], ALONG_COLS) + dot(grad_up, weights_in[1], ALONG_COLS)
        full_rows = scatter_rest(parts.reshape(blocks, capacity, width), "expert", 0)[0].astype(BF16)
        return (dot(second_select, full_rows, ALONG_ROWS).astype(BF16)[None], mirror[None])

    input_grad, mirror = lax.cond(over[0] > 0, full_case, packed_case, grad_rows, mirror_packed, info)
    return (first_output[None], input_grad, mirror)


def solution(mesh):
    tokens = P("pipe", "expert", None)
    columns = P("pipe", None, None, "expert")
    return jax.shard_map(
        body,
        mesh=mesh,
        in_specs=(
            tokens,
            tokens,
            tokens,
            P("pipe", None),
            columns,
            tokens,
            tokens,
            tokens,
            tokens,
            columns,
        ),
        out_specs=(tokens, tokens, columns),
        check_vma=False,
    )
```
